32 devices in a mesh: clip: 4 (over z), tm: 4 (over x, core), tile: 2 (over y).
Axes of the slice: x: 2, y: 2, z: 4, core: 2. Of those that a mesh axis runs over, the one named last changes fastest.
Arguments:
- activation: bfloat16 [4, 8, 4, 32, 384], P('clip', 'tm', 'tile'), may hold values from -6 to 6
- cotangent: bfloat16 [4, 8, 4, 32, 384], P('clip', 'tm', 'tile'), may hold values from -6 to 6
- kernel_weight: bfloat16 [3, 3, 3, 384, 384], replicated, may hold values from -0.0625 to 0.0625
Outputs:
- input_grad: bfloat16 [4, 8, 4, 32, 384], P('clip', 'tm', 'tile')
- weight_grad: float32 [3, 3, 3, 384, 384], P(None, None, None, 'tile', ('clip', 'tm'))
The draws below stay inside these ranges and needn't reach their ends.
All inputs are finite; a program needn't handle non-finite values.
Results may differ from the reference program's by a relative error of at most 0.003.
Values may be sent and summed in bfloat16 or wider, within the bound.
No kernel may reach another device: no remote copies, remote signals or barrier semaphores. Data moves between devices by JAX's collectives and lax.ppermute only.
A program may use at most 128 MiB of HBM per device.

```python
import math
import jax
import jax.numpy as jnp
from jax import lax

C = 384
WIDTH = 32
CLIPS = 4
FRAMES = 8
HEIGHT = 4
CELLS = 4096


def levels(key, dims, pieces, low, top_value):
    factor_of, own = 1.0, jax.random.fold_in(key, 6)
    for position, blocks in pieces:
        draws = jnp.exp(jax.random.uniform(jax.random.fold_in(own, position), (blocks,), jnp.float32, low / len(pieces), top_value / len(pieces)))
        factor_of = factor_of * jnp.repeat(draws, dims[position] // blocks).reshape([-1 if axis == position else 1 for axis in range(len(dims))])
    return factor_of


def gaussian(rng, dims, deviation, limit, split=(), kind=jnp.bfloat16):
    result = jax.random.normal(rng, dims, jnp.float32) * deviation
    if len(split) > 0:
        result = levels(rng, dims, split, -0.22, 0.18) * result
    return jnp.clip(result, min=-limit, max=limit).astype(kind)


def setup_inputs(seed: int = 0) -> dict:
    key_of = jax.random.split(jax.random.key(seed), 4)
    activation = gaussian(key_of[0], (CLIPS, FRAMES, HEIGHT, WIDTH, C), 1.0, 6.0, ((0, 4), (1, 4), (2, 2)))
    cotangent = gaussian(key_of[1], (CLIPS, FRAMES, HEIGHT, WIDTH, C), 1.0, 6.0, ((0, 4), (1, 4), (2, 2)))
    kernel_weight = gaussian(key_of[2], (3, 3, 3, C, C), (27 * C) ** -0.5, 0.0625)
    return {"activation": activation, "cotangent": cotangent, "kernel_weight": kernel_weight}


NUMBERS = ('NDHWC', 'DHWOI', 'NDHWC')

def reference(activation, cotangent, kernel_weight):
    pre_value = activation.astype(jnp.float32)
    logistic = jax.nn.sigmoid(pre_value)
    silu_out = (pre_value * logistic).astype(jnp.bfloat16)
    flipped = jnp.flip(kernel_weight, (0, 1, 2)).astype(jnp.float32)
    padded_cot = jnp.pad(cotangent.astype(jnp.float32), ((0, 0), (0, 2), (1, 1), (1, 1), (0, 0)))
    back = lax.conv_general_dilated(padded_cot, flipped, (1, 1, 1), 'VALID', dimension_numbers=NUMBERS, precision=lax.Precision.HIGHEST)
    input_grad = (back * logistic * (1.0 + pre_value * (1.0 - logistic))).astype(jnp.bfloat16)
    padded_silu = jnp.pad(silu_out.astype(jnp.float32), ((0, 0), (2, 0), (1, 1), (1, 1), (0, 0)))
    frames = activation.shape[1]
    height = activation.shape[2]
    columns = activation.shape[3]
    channels = activation.shape[4]
    flat_cot = cotangent.astype(jnp.float32).reshape(-1, channels)
    products = []
    for time_tap in range(3):
        for row_tap in range(3):
            for column_tap in range(3):
                window = padded_silu[:, time_tap:time_tap + frames, row_tap:row_tap + height, column_tap:column_tap + columns]
                window = window.reshape(-1, channels)
                products.append(jnp.dot(window.T, flat_cot, precision=lax.Precision.HIGHEST))
    weight_grad = jnp.stack(products).reshape(3, 3, 3, channels, channels) / math.sqrt(CELLS)
    return (input_grad, weight_grad)
```

```python
import math

import jax
import jax.numpy as jnp
from jax import lax
from jax.experimental import pallas as pl
from jax.experimental.pallas import tpu as pltpu
from jax.sharding import PartitionSpec as P

NUMBERS = ("NDHWC", "DHWOI", "NDHWC")
AXES = ("clip", "tm", "tile")
TAPS = 3
LANES = 128


def passed_along(value, axis, steps):
    count = lax.axis_size(axis)
    leading, last = (max(0, -steps), min(count, count - steps))
    return lax.ppermute(value, axis, [(source, source + steps) for source in range(leading, last)])


def tap_product(left_rows, right_rows):
    return lax.dot_general(
        left_rows, right_rows, (((0,), (0,)), ((), ())), preferred_element_type=jnp.float32
    )


def general_plan(activation, cotangent, kernel_weight):
    frames = activation.shape[1]
    height = activation.shape[2]
    columns = activation.shape[3]
    channels = activation.shape[4]
    pre_value = activation.astype(jnp.float32)
    logistic = jax.nn.sigmoid(pre_value)
    silu_out = (pre_value * logistic).astype(jnp.bfloat16)
    future = passed_along(cotangent, "tm", -1)
    cot_ext = jnp.concatenate([cotangent, future], axis=1)
    products = []
    total_cells = (
        lax.axis_size("clip")
        * lax.axis_size("tm")
        * lax.axis_size("tile")
        * activation.shape[0]
        * frames
        * height
        * columns
    )
    whole_cot = lax.all_gather(cot_ext, "tile", axis=2, tiled=True)
    padded_all = jnp.pad(whole_cot, ((0, 0), (0, 0), (1, 1), (1, 1), (0, 0)))
    all_rows = whole_cot.shape[2]
    row_start = lax.axis_index("tile") * height
    padded_cot = lax.dynamic_slice_in_dim(padded_all, row_start, height + 2, 2)
    silu_block = lax.all_to_all(silu_out, "tile", split_axis=4, concat_axis=2, tiled=True)
    block_width = silu_block.shape[4]
    flat_block = silu_block.reshape(-1, block_width)
    for time_tap in range(3):
        for row_tap in range(3):
            for column_tap in range(3):
                window = padded_all[
                    :,
                    2 - time_tap : 2 - time_tap + frames,
                    2 - row_tap : 2 - row_tap + all_rows,
                    2 - column_tap : 2 - column_tap + columns,
                ]
                products.append(tap_product(flat_block, window.reshape(-1, channels)))
    partial_grad = jnp.stack(products).reshape(3, 3, 3, block_width, channels)
    reduced = lax.psum_scatter(partial_grad, ("clip", "tm"), scatter_dimension=4, tiled=True)
    back = lax.conv_general_dilated(
        padded_cot,
        jnp.flip(kernel_weight, (0, 1, 2)),
        (1, 1, 1),
        "VALID",
        dimension_numbers=NUMBERS,
        preferred_element_type=jnp.float32,
    )
    input_grad = (back * logistic * (1.0 + pre_value * (1.0 - logistic))).astype(jnp.bfloat16)
    return (input_grad, reduced / math.sqrt(total_cells))


class Sizes:
    def __init__(self, mesh_shape, shape):
        self.clips, self.tms, self.tiles = (mesh_shape[axis] for axis in AXES)
        self.batch, self.frames, self.height, self.columns, self.channels = shape
        self.pairs = self.tms // 2
        self.cells = self.frames * self.height * self.columns
        self.frame_cells = self.tiles * self.height * self.columns
        self.rows = self.channels // self.tiles
        self.block = self.channels // self.clips
        self.wide = self.block // self.pairs
        self.narrow = self.wide // 2
        self.group = self.rows + self.wide
        self.payload = self.channels + self.block
        self.total = self.clips * self.tms * self.tiles * self.batch * self.cells

    def fits(self):
        return (
            self.batch == 1
            and self.tiles == 2
            and self.tms == 4
            and self.frames == 2
            and self.clips & (self.clips - 1) == 0
            and self.cells == LANES
            and self.frame_cells == LANES
            and self.channels % (self.tiles * self.clips * self.tms) == 0
            and self.rows % 16 == 0
            and self.wide % 16 == 0
            and self.narrow % 8 == 0
        )


def exchange(size, value, clip=0, pair=0, core=0, tile=0):
    def place(z, x, c, y):
        return (z * size.tms + x * 2 + c) * size.tiles + y

    moves = [
        (place(z, x, c, y), place(z ^ clip, x ^ pair, c ^ core, y ^ tile))
        for z in range(size.clips)
        for x in range(size.pairs)
        for c in range(2)
        for y in range(size.tiles)
    ]
    return lax.ppermute(value, AXES, moves)


def position(size):
    tm = lax.axis_index("tm")
    return lax.axis_index("clip"), tm // 2, tm % 2, lax.axis_index("tile")


def prepare(size, activation, cotangent):
    def body(act_ref, cot_ref, *refs):
        outs, silu_t, cot_t = refs[:-2], refs[-2], refs[-1]
        z, x, c, y = position(size)
        pre_value = act_ref[...].astype(jnp.float32)
        silu = pre_value * jax.nn.sigmoid(pre_value)
        silu_t[...] = silu.T.astype(jnp.bfloat16)
        cot_t[...] = cot_ref[...].astype(jnp.float32).T.astype(jnp.bfloat16)

        def cut(ref, start, count, step):
            return ref[pl.ds(pl.multiple_of(start, step), count), :]

        rows, wide, group = size.rows, size.wide, size.group
        for mask, out in enumerate(outs):
            first = jnp.bitwise_xor(z, mask) * size.block
            out[0:rows, :] = cut(silu_t, (1 - y) * rows, rows, 16)
            out[rows:group, :] = cut(cot_t, first + x * wide, wide, 16)
            out[group : group + rows, :] = cut(silu_t, y * rows, rows, 16)
            out[group + rows :, :] = cut(cot_t, first + (1 - x) * wide, wide, 16)

    shape = jax.ShapeDtypeStruct((size.payload, LANES), jnp.bfloat16)
    return pl.pallas_call(
        body,
        out_shape=[shape] * size.clips,
        in_specs=[pl.BlockSpec(memory_space=pltpu.VMEM)] * 2,
        out_specs=[pl.BlockSpec(memory_space=pltpu.VMEM)] * size.clips,
        scratch_shapes=[pltpu.VMEM((size.channels, LANES), jnp.bfloat16)] * 2,
        name="prepare",
    )(activation.reshape(size.cells, size.channels), cotangent.reshape(size.cells, size.channels))


def pieces(size, blocks):
    rows, group = size.rows, size.group
    to_tile = jnp.concatenate([block[:group] for block in blocks])
    to_pair = jnp.concatenate([block[group:] for block in blocks])
    to_both = jnp.concatenate(
        [part for block in blocks for part in (block[:rows], block[group + rows :])]
    )
    return to_tile, to_pair, to_both


def products(size, blocks, near, swapped):
    rows, wide, group = size.rows, size.wide, size.group
    window = TAPS * TAPS
    held = 2 * size.pairs + 2 * size.pairs
    all_frames = size.frames * size.tms
    flat_near = [array for arrays in near for array in arrays]

    def body(*refs):
        block_refs = refs[: size.clips]
        near_refs = refs[size.clips : size.clips + len(flat_near)]
        swap_ref = refs[size.clips + len(flat_near)]
        keep_ref, send_ref, silu_ref, cot_ref, shift_ref, sum_ref = refs[-6:]
        z, x, c, y = position(size)
        lane = lax.broadcasted_iota(jnp.int32, (wide, LANES), 1)
        row, column = lane // size.columns, lane % size.columns
        last_row = size.tiles * size.height - 1
        half = LANES // 2

        def by_frame(own, other):
            low = jnp.where(y == 0, own, other)
            high = jnp.where(y == 0, other, own)
            return (
                jnp.concatenate([low[:, :half], high[:, :half]], axis=1),
                jnp.concatenate([low[:, half:], high[:, half:]], axis=1),
            )

        zero = jnp.zeros((wide, LANES), jnp.float32)
        for extra in range(2):
            cot_ref[all_frames + extra] = zero
        sum_ref[...] = jnp.zeros_like(sum_ref)
        for clip in range(size.clips):
            block = block_refs[clip]
            where = 0
            while where < len(near) and clip >= where_end(near, where, group):
                where += 1
            at = (clip - (where_end(near, where - 1, group) if where else 0)) * group
            tile_ref, pair_ref, both_ref = near_refs[where * 3 : where * 3 + 3]
            silu_parts = [block[group : group + rows, :]] + [
                ref[at : at + rows, :] for ref in (tile_ref, pair_ref, both_ref)
            ]
            cot_parts = [block[rows:group, :]] + [
                ref[at + rows : at + group, :] for ref in (tile_ref, pair_ref, both_ref)
            ]
            base = clip * 4 * wide
            swap_parts = [swap_ref[base + part * wide : base + (part + 1) * wide, :] for part in range(4)]
            for side in range(2):
                pair = x if side == 0 else 1 - x
                first, second = by_frame(*silu_parts[2 * side : 2 * side + 2])
                silu_ref[pair, :, 0:LANES] = first
                silu_ref[pair, :, LANES:] = second
                for core, parts in ((c, cot_parts), (1 - c, swap_parts)):
                    wide_parts = [part.astype(jnp.float32) for part in parts[2 * side : 2 * side + 2]]
                    first, second = by_frame(*wide_parts)
                    frame = pair * 2 * size.frames + core * size.frames
                    cot_ref[frame] = first
                    cot_ref[frame + 1] = second
            for frame in range(held):
                value = cot_ref[c * size.frames + frame]
                for row_tap in range(TAPS):
                    for column_tap in range(TAPS):
                        down, right = 1 - row_tap, 1 - column_tap
                        moved = value
                        step = down * size.columns + right
                        if step:
                            moved = pltpu.roll(value, (-step) % LANES, 1)
                        inside = (
                            (row + down >= 0)
                            & (row + down <= last_row)
                            & (column + right >= 0)
                            & (column + right < size.columns)
                        )
                        moved = jnp.where(inside, moved, 0.0)
                        tap = (row_tap * TAPS + column_tap) * wide
                        shift_ref[tap : tap + wide, frame * LANES : (frame + 1) * LANES] = (
                            moved.astype(jnp.bfloat16)
                        )
            for time_tap in range(TAPS):
                later = TAPS - 1 - time_tap
                total = sum_ref[time_tap]
                for pair in range(size.pairs):
                    start = (pair * 2 * size.frames + later) * LANES
                    total += lax.dot_general(
                        shift_ref[:, start : start + size.frames * LANES],
                        silu_ref[pair],
                        (((1,), (1,)), ((), ())),
                        preferred_element_type=jnp.float32,
                    )
                sum_ref[time_tap] = total
        for time_tap in range(TAPS):
            for tap in range(window):
                for out, core in ((keep_ref, c), (send_ref, 1 - c)):
                    start = pl.multiple_of(tap * wide + core * size.narrow, 8)
                    out[time_tap * window + tap] = sum_ref[time_tap, pl.ds(start, size.narrow), :]

    shape = jax.ShapeDtypeStruct((TAPS * window, size.narrow, rows), jnp.float32)
    operands = list(blocks) + flat_near + [swapped]
    return pl.pallas_call(
        body,
        out_shape=[shape, shape],
        in_specs=[pl.BlockSpec(memory_space=pltpu.VMEM)] * len(operands),
        out_specs=[pl.BlockSpec(memory_space=pltpu.VMEM)] * 2,
        scratch_shapes=[
            pltpu.VMEM((size.pairs, rows, size.frames * LANES), jnp.bfloat16),
            pltpu.VMEM((all_frames + 2, wide, LANES), jnp.float32),
            pltpu.VMEM((window * wide, held * LANES), jnp.bfloat16),
            pltpu.VMEM((TAPS, window * wide, rows), jnp.float32),
        ],
        name="products",
    )(*operands)


def where_end(near, index, group):
    return sum(arrays[0].shape[0] // group for arrays in near[: index + 1])


def finish(size, mine, theirs):
    root = math.sqrt(size.total)

    def body(mine_ref, theirs_ref, out_ref):
        for tap in range(mine.shape[0]):
            out_ref[tap] = ((mine_ref[tap] + theirs_ref[tap]) / root).T

    return pl.pallas_call(
        body,
        out_shape=jax.ShapeDtypeStruct((mine.shape[0], size.rows, size.narrow), jnp.float32),
        in_specs=[pl.BlockSpec(memory_space=pltpu.VMEM)] * 2,
        out_specs=pl.BlockSpec(memory_space=pltpu.VMEM),
        name="finish",
    )(mine, theirs)


def gather_plan(size, activation, cotangent, kernel_weight):
    rows, wide, group = size.rows, size.wide, size.group
    y = lax.axis_index("tile")
    blocks = prepare(size, activation, cotangent)
    moved = {mask: exchange(size, blocks[mask], clip=mask) for mask in range(size.clips - 1, 0, -1)}
    arrived = [blocks[0]] + [moved[mask] for mask in range(1, size.clips)]
    near = []
    for part in (arrived[:-1], arrived[-1:]):
        to_tile, to_pair, to_both = pieces(size, part)
        near.append(
            (
                exchange(size, to_tile, tile=1),
                exchange(size, to_pair, pair=1),
                exchange(size, to_both, pair=1, tile=1),
            )
        )
    cot_parts = []
    for clip, block in enumerate(arrived):
        where = 0 if clip < size.clips - 1 else 1
        at = (clip if where == 0 else 0) * group
        cot_parts.append(block[rows:group])
        cot_parts += [array[at + rows : at + group] for array in near[where]]
    swapped = exchange(size, jnp.concatenate(cot_parts), core=1)

    edge = lax.dynamic_slice_in_dim(cotangent, (size.height - 1) * (1 - y), 1, 2)
    edge = exchange(size, edge, tile=1)
    blank = jnp.zeros_like(edge)
    with_halo = jnp.concatenate(
        [jnp.where(y == 0, blank, edge), cotangent, jnp.where(y == 0, edge, blank)], axis=2
    )
    later = passed_along(with_halo, "tm", -1)
    padded = jnp.pad(
        jnp.concatenate([with_halo, later], axis=1), ((0, 0), (0, 0), (0, 0), (1, 1), (0, 0))
    )
    back = lax.conv_general_dilated(
        padded,
        jnp.flip(kernel_weight, (0, 1, 2)),
        (1, 1, 1),
        "VALID",
        dimension_numbers=NUMBERS,
        preferred_element_type=jnp.float32,
    )
    pre_value = activation.astype(jnp.float32)
    logistic = jax.nn.sigmoid(pre_value)
    input_grad = (back * logistic * (1.0 + pre_value * (1.0 - logistic))).astype(jnp.bfloat16)

    keep, send = products(size, arrived, near, swapped)
    weight = finish(size, keep, exchange(size, send, core=1))
    return input_grad, weight.reshape(TAPS, TAPS, TAPS, rows, size.narrow)


def solution(mesh):
    in_specs = (P("clip", "tm", "tile", None, None), P("clip", "tm", "tile", None, None), P())
    out_specs = (P("clip", "tm", "tile", None, None), P(None, None, None, "tile", ("clip", "tm")))

    def on_device(activation, cotangent, kernel_weight):
        size = Sizes(mesh.shape, activation.shape)
        if size.fits():
            return gather_plan(size, activation, cotangent, kernel_weight)
        return general_plan(activation, cotangent, kernel_weight)

    return jax.shard_map(
        on_device, mesh=mesh, in_specs=in_specs, out_specs=out_specs, check_vma=False
    )
```

```python
import math

import jax
import jax.numpy as jnp
from jax import lax
from jax.experimental import pallas as pl
from jax.experimental.pallas import tpu as pltpu
from jax.sharding import PartitionSpec as P


NUMBERS = ("NDHWC", "DHWOI", "NDHWC")
AXES = ("clip", "tm", "tile")
TAPS = 3
LANES = 128
GRANT = 16 * 1024 * 1024
PREPARE = 1 << 33


def passed_along(value, axis, steps):
    count = lax.axis_size(axis)
    leading, last = (max(0, -steps), min(count, count - steps))
    return lax.ppermute(value, axis, [(source, source + steps) for source in range(leading, last)])


def tap_product(left_rows, right_rows):
    return lax.dot_general(
        left_rows, right_rows, (((0,), (0,)), ((), ())), preferred_element_type=jnp.float32
    )


def general_plan(activation, cotangent, kernel_weight):
    frames = activation.shape[1]
    height = activation.shape[2]
    columns = activation.shape[3]
    channels = activation.shape[4]
    pre_value = activation.astype(jnp.float32)
    logistic = jax.nn.sigmoid(pre_value)
    silu_out = (pre_value * logistic).astype(jnp.bfloat16)
    future = passed_along(cotangent, "tm", -1)
    cot_ext = jnp.concatenate([cotangent, future], axis=1)
    products = []
    total_cells = (
        lax.axis_size("clip")
        * lax.axis_size("tm")
        * lax.axis_size("tile")
        * activation.shape[0]
        * frames
        * height
        * columns
    )
    whole_cot = lax.all_gather(cot_ext, "tile", axis=2, tiled=True)
    padded_all = jnp.pad(whole_cot, ((0, 0), (0, 0), (1, 1), (1, 1), (0, 0)))
    all_rows = whole_cot.shape[2]
    row_start = lax.axis_index("tile") * height
    padded_cot = lax.dynamic_slice_in_dim(padded_all, row_start, height + 2, 2)
    silu_block = lax.all_to_all(silu_out, "tile", split_axis=4, concat_axis=2, tiled=True)
    block_width = silu_block.shape[4]
    flat_block = silu_block.reshape(-1, block_width)
    for time_tap in range(3):
        for row_tap in range(3):
            for column_tap in range(3):
                window = padded_all[
                    :,
                    2 - time_tap : 2 - time_tap + frames,
                    2 - row_tap : 2 - row_tap + all_rows,
                    2 - column_tap : 2 - column_tap + columns,
                ]
                products.append(tap_product(flat_block, window.reshape(-1, channels)))
    partial_grad = jnp.stack(products).reshape(3, 3, 3, block_width, channels)
    reduced = lax.psum_scatter(partial_grad, ("clip", "tm"), scatter_dimension=4, tiled=True)
    back = lax.conv_general_dilated(
        padded_cot,
        jnp.flip(kernel_weight, (0, 1, 2)),
        (1, 1, 1),
        "VALID",
        dimension_numbers=NUMBERS,
        preferred_element_type=jnp.float32,
    )
    input_grad = (back * logistic * (1.0 + pre_value * (1.0 - logistic))).astype(jnp.bfloat16)
    return (input_grad, reduced / math.sqrt(total_cells))


class Sizes:
    def __init__(self, mesh_shape, shape):
        self.clips, self.tms, self.tiles = (mesh_shape[axis] for axis in AXES)
        self.batch, self.frames, self.height, self.columns, self.channels = shape
        self.pairs = self.tms // 2
        self.cells = self.frames * self.height * self.columns
        self.frame_cells = self.tiles * self.height * self.columns
        self.rows = self.channels // self.tiles
        self.block = self.channels // self.clips
        self.wide = self.block // self.pairs
        self.narrow = self.wide // 2
        self.group = self.rows + self.wide
        self.payload = self.channels + self.block
        self.total = self.clips * self.tms * self.tiles * self.batch * self.cells

    def fits(self):
        return (
            self.batch == 1
            and self.tiles == 2
            and self.tms == 4
            and self.frames == 2
            and self.clips & (self.clips - 1) == 0
            and self.cells == LANES
            and self.frame_cells == LANES
            and self.channels % (self.tiles * self.clips * self.tms) == 0
            and self.rows % 16 == 0
            and self.wide % 16 == 0
            and self.narrow % 8 == 0
        )


def exchange(size, value, clip=0, pair=0, core=0, tile=0):
    def place(z, x, c, y):
        return (z * size.tms + x * 2 + c) * size.tiles + y

    moves = [
        (place(z, x, c, y), place(z ^ clip, x ^ pair, c ^ core, y ^ tile))
        for z in range(size.clips)
        for x in range(size.pairs)
        for c in range(2)
        for y in range(size.tiles)
    ]
    return lax.ppermute(value, AXES, moves)


def position():
    tm = lax.axis_index("tm")
    return lax.axis_index("clip"), tm // 2, tm % 2, lax.axis_index("tile")


def prepare(size, activation, cotangent):
    width = size.columns
    fold = size.channels // 2

    def body(act_hbm, cot_hbm, *refs):
        outs, turned_ref, edge_ref, act_ref = refs[: size.clips], *refs[size.clips : size.clips + 3]
        cot_ref, silu_t, sems = refs[size.clips + 3 :]
        copies = [
            pltpu.make_async_copy(act_hbm, act_ref, sems.at[0]),
            pltpu.make_async_copy(cot_hbm, cot_ref, sems.at[1]),
        ]
        for copy in copies:
            copy.start()
        z, x, _, y = position()
        copies[0].wait()
        pre_value = act_ref[...].astype(jnp.float32)
        silu = pre_value * jax.nn.sigmoid(pre_value)
        silu_t[...] = silu.T.astype(jnp.bfloat16)
        copies[1].wait()
        turned = cot_ref[...].astype(jnp.float32).T
        turned_ref[...] = turned.astype(jnp.bfloat16)
        rowed = turned.reshape(size.channels, LANES)
        near = jnp.where(y == 0, rowed, pltpu.roll(rowed, width, 1))
        first = near[:, width : 2 * width]
        second = near[:, 3 * width : 4 * width]
        edge_ref[...] = jnp.concatenate(
            [first[:fold], second[:fold], first[fold:], second[fold:]], axis=1
        ).astype(jnp.bfloat16)

        def cut(ref, start, count, step):
            return ref[pl.ds(pl.multiple_of(start, step), count), :]

        rows, wide, group = size.rows, size.wide, size.group
        for mask, out in enumerate(outs):
            first = jnp.bitwise_xor(z, mask) * size.block
            out[0:rows, :] = cut(silu_t, (1 - y) * rows, rows, 16)
            out[rows:group, :] = cut(turned_ref, first + x * wide, wide, 16)
            out[group : group + rows, :] = cut(silu_t, y * rows, rows, 16)
            out[group + rows :, :] = cut(turned_ref, first + (1 - x) * wide, wide, 16)

    shape = jax.ShapeDtypeStruct((size.payload, LANES), jnp.bfloat16)
    flat = jax.ShapeDtypeStruct((size.channels, LANES), jnp.bfloat16)
    folded = jax.ShapeDtypeStruct((fold, LANES), jnp.bfloat16)
    as_given = jax.ShapeDtypeStruct((size.cells, size.channels), jnp.bfloat16)
    return pl.pallas_call(
        body,
        out_shape=[shape] * size.clips + [flat, folded, as_given],
        in_specs=[pl.BlockSpec(memory_space=pltpu.MemorySpace.HBM)] * 2,
        out_specs=[pl.BlockSpec(memory_space=pltpu.VMEM)] * (size.clips + 3),
        scratch_shapes=[
            pltpu.VMEM((size.cells, size.channels), jnp.bfloat16),
            pltpu.VMEM((size.channels, LANES), jnp.bfloat16),
            pltpu.SemaphoreType.DMA((2,)),
        ],
        compiler_params=pltpu.CompilerParams(vmem_limit_bytes=GRANT),
        cost_estimate=pl.CostEstimate(
            flops=PREPARE, bytes_accessed=4 * activation.size, transcendentals=activation.size
        ),
        name="prepare",
    )(
        in_hbm(activation.reshape(size.cells, size.channels)),
        in_hbm(cotangent.reshape(size.cells, size.channels)),
    )


def in_hbm(value):
    return pltpu.with_memory_space_constraint(value, pltpu.MemorySpace.HBM)


def input_gradient(size, activation, halo, later, kernel_weight):
    width, channels = size.columns, size.channels
    window = TAPS * TAPS
    lanes = size.frames * LANES

    def body(act_ref, halo_ref, later_ref, weight_ref, out_ref, moved_ref, sum_ref):
        y = lax.axis_index("tile")
        lane = lax.broadcasted_iota(jnp.int32, (channels, LANES), 1)
        column, row = lane % width, lane // width
        side = jnp.where(y == 0, 3, 0)

        def shift(frame):
            source = halo_ref if frame < size.frames else later_ref
            at = frame % size.frames
            value = source[:channels, :].astype(jnp.float32)
            folded = source[channels:, :].astype(jnp.float32)
            edge = jnp.concatenate([folded, pltpu.roll(folded, LANES // 2, 1)], axis=0)
            own = pltpu.roll(value, (width - at * 2 * width) % LANES, 1)
            up = pltpu.roll(edge, (-at * width) % LANES, 1)
            down = pltpu.roll(edge, ((3 - at) * width) % LANES, 1)
            beside = jnp.where(y == 0, down, up)
            middle = (row == 1) | (row == 2)
            strip = jnp.where(middle, own, jnp.where(row == side, beside, 0.0))
            for row_tap in range(TAPS):
                for column_tap in range(TAPS):
                    below, right = 1 - row_tap, 1 - column_tap
                    step = below * width + right
                    moved = pltpu.roll(strip, (-step) % LANES, 1) if step else strip
                    if right:
                        moved = jnp.where(column != (width - 1 if right > 0 else 0), moved, 0.0)
                    tap = (row_tap * TAPS + column_tap) * channels
                    moved_ref[tap : tap + channels, frame * LANES : (frame + 1) * LANES] = (
                        moved.astype(jnp.bfloat16)
                    )

        shift(0)
        for delay in range(TAPS):
            shift(delay + 1)
            first = (TAPS - 1 - delay) * window
            for row_tap in range(TAPS):
                tap = row_tap * TAPS
                weights = [weight_ref[first + tap + column_tap] for column_tap in range(TAPS)]
                term = jnp.dot(
                    jnp.concatenate(weights, axis=1),
                    moved_ref[
                        tap * channels : (tap + TAPS) * channels,
                        delay * LANES : delay * LANES + lanes,
                    ],
                    preferred_element_type=jnp.float32,
                )
                if delay == 0 and row_tap == 0:
                    sum_ref[...] = term
                else:
                    sum_ref[...] += term
        first = pltpu.roll(sum_ref[:, :LANES], LANES - width, 1)
        second = pltpu.roll(sum_ref[:, LANES:], width, 1)
        back = jnp.where(lane < 2 * width, first, second).T
        pre_value = act_ref[...].astype(jnp.float32)
        logistic = jax.nn.sigmoid(pre_value)
        out_ref[...] = (back * logistic * (1.0 + pre_value * (1.0 - logistic))).astype(jnp.bfloat16)

    return pl.pallas_call(
        body,
        out_shape=jax.ShapeDtypeStruct((size.cells, channels), jnp.bfloat16),
        in_specs=[pl.BlockSpec(memory_space=pltpu.VMEM)] * 4,
        out_specs=pl.BlockSpec(memory_space=pltpu.VMEM),
        scratch_shapes=[
            pltpu.VMEM((window * channels, 2 * lanes), jnp.bfloat16),
            pltpu.VMEM((channels, lanes), jnp.float32),
        ],
        compiler_params=pltpu.CompilerParams(vmem_limit_bytes=GRANT),
        cost_estimate=pl.CostEstimate(
            flops=2 * TAPS * window * channels * channels * lanes,
            bytes_accessed=2 * kernel_weight.size,
            transcendentals=activation.size,
        ),
        name="input_gradient",
    )(activation, halo, later, kernel_weight.reshape(TAPS * window, channels, channels))


def pieces(size, blocks):
    rows, group = size.rows, size.group
    to_tile = jnp.concatenate([block[:group] for block in blocks])
    to_pair = jnp.concatenate([block[group:] for block in blocks])
    to_both = jnp.concatenate(
        [part for block in blocks for part in (block[:rows], block[group + rows :])]
    )
    return to_tile, to_pair, to_both


def products(size, blocks, near, swapped, before):
    rows, wide, group = size.rows, size.wide, size.group
    window = TAPS * TAPS
    held = size.pairs * 2 * size.frames
    all_frames = size.frames * size.tms
    first = before is None

    def body(*refs):
        refs = list(refs)
        block_refs = [refs.pop(0) for _ in blocks]
        tile_ref, pair_ref, both_ref, swap_ref = (refs.pop(0) for _ in range(4))
        before_ref = None if first else refs.pop(0)
        silu_ref, cot_ref, shift_ref = refs[-3:]
        _, x, c, y = position()
        lane = lax.broadcasted_iota(jnp.int32, (wide, LANES), 1)
        row, column = lane // size.columns, lane % size.columns
        last_row = size.tiles * size.height - 1
        half = LANES // 2

        def by_frame(own, other):
            low = jnp.where(y == 0, own, other)
            high = jnp.where(y == 0, other, own)
            return (
                jnp.concatenate([low[:, :half], high[:, :half]], axis=1),
                jnp.concatenate([low[:, half:], high[:, half:]], axis=1),
            )

        zero = jnp.zeros((wide, LANES), jnp.float32)
        for extra in range(2):
            cot_ref[all_frames + extra] = zero
        for clip, block in enumerate(block_refs):
            at = clip * group
            others = (tile_ref, pair_ref, both_ref)
            silu_parts = [block[group : group + rows, :]] + [ref[at : at + rows, :] for ref in others]
            cot_parts = [block[rows:group, :]] + [ref[at + rows : at + group, :] for ref in others]
            base = clip * 4 * wide
            swap_parts = [swap_ref[base + part * wide : base + (part + 1) * wide, :] for part in range(4)]
            for side in range(2):
                pair = x if side == 0 else 1 - x
                early, later = by_frame(*silu_parts[2 * side : 2 * side + 2])
                silu_ref[clip, pair, :, 0:LANES] = early
                silu_ref[clip, pair, :, LANES:] = later
                for core, parts in ((c, cot_parts), (1 - c, swap_parts)):
                    wide_parts = [part.astype(jnp.float32) for part in parts[2 * side : 2 * side + 2]]
                    early, later = by_frame(*wide_parts)
                    frame = pair * 2 * size.frames + core * size.frames
                    cot_ref[frame] = early
                    cot_ref[frame + 1] = later
            for frame in range(held):
                value = cot_ref[c * size.frames + frame]
                for row_tap in range(TAPS):
                    for column_tap in range(TAPS):
                        down, right = 1 - row_tap, 1 - column_tap
                        moved = value
                        step = down * size.columns + right
                        if step:
                            moved = pltpu.roll(value, (-step) % LANES, 1)
                        inside = (
                            (row + down >= 0)
                            & (row + down <= last_row)
                            & (column + right >= 0)
                            & (column + right < size.columns)
                        )
                        moved = jnp.where(inside, moved, 0.0)
                        tap = (row_tap * TAPS + column_tap) * wide
                        shift_ref[clip, tap : tap + wide, frame * LANES : (frame + 1) * LANES] = (
                            moved.astype(jnp.bfloat16)
                        )
        for time_tap in range(TAPS):
            later = TAPS - 1 - time_tap
            total = None if first else before_ref[time_tap]
            for clip in range(len(blocks)):
                for pair in range(size.pairs):
                    start = (pair * 2 * size.frames + later) * LANES
                    term = lax.dot_general(
                        shift_ref[clip, :, start : start + size.frames * LANES],
                        silu_ref[clip, pair],
                        (((1,), (1,)), ((), ())),
                        preferred_element_type=jnp.float32,
                    )
                    total = term if total is None else total + term
            if first:
                refs[0][time_tap] = total
                continue
            sum_ref = refs[2]
            sum_ref[...] = total
            for tap in range(window):
                for out, core in ((refs[0], c), (refs[1], 1 - c)):
                    start = pl.multiple_of(tap * wide + core * size.narrow, 8)
                    out[time_tap * window + tap] = sum_ref[pl.ds(start, size.narrow), :]

    scratch = [
        pltpu.VMEM((len(blocks), size.pairs, rows, size.frames * LANES), jnp.bfloat16),
        pltpu.VMEM((all_frames + 2, wide, LANES), jnp.float32),
        pltpu.VMEM((len(blocks), window * wide, held * LANES), jnp.bfloat16),
    ]
    operands = list(blocks) + list(near) + [swapped]
    if first:
        shapes = jax.ShapeDtypeStruct((TAPS, window * wide, rows), jnp.float32)
        outs = pl.BlockSpec(memory_space=pltpu.VMEM)
    else:
        shapes = [jax.ShapeDtypeStruct((TAPS * window, size.narrow, rows), jnp.float32)] * 2
        outs = [pl.BlockSpec(memory_space=pltpu.VMEM)] * 2
        operands.append(before)
        scratch.insert(0, pltpu.VMEM((window * wide, rows), jnp.float32))
    return pl.pallas_call(
        body,
        out_shape=shapes,
        in_specs=[pl.BlockSpec(memory_space=pltpu.VMEM)] * len(operands),
        out_specs=outs,
        scratch_shapes=scratch,
        compiler_params=pltpu.CompilerParams(vmem_limit_bytes=GRANT),
        cost_estimate=pl.CostEstimate(
            flops=2 * TAPS * window * wide * rows * len(blocks) * size.pairs * 2 * LANES,
            bytes_accessed=4 * TAPS * window * wide * rows,
            transcendentals=0,
        ),
        name="early_products" if first else "late_products",
    )(*operands)


def gather_plan(size, activation, cotangent, kernel_weight):
    rows, group = size.rows, size.group
    *blocks, turned, edge, near_act = prepare(size, activation, cotangent)
    arrived = [blocks[0]]
    for mask in range(1, size.clips):
        arrived.append(exchange(size, blocks[mask], clip=mask))
    edge = exchange(size, edge, tile=1)
    halo = jnp.concatenate([turned, edge])
    later = passed_along(halo, "tm", -1)
    input_grad = input_gradient(size, near_act, halo, later, kernel_weight)
    input_grad = input_grad.reshape(activation.shape)

    half = size.clips - 1
    total = None
    for part in (arrived[:half], arrived[half:]):
        to_tile, to_pair, to_both = pieces(size, part)
        near = []
        for value, bits in (
            (to_tile, {"tile": 1}), (to_pair, {"pair": 1}), (to_both, {"pair": 1, "tile": 1})
        ):
            near.append(exchange(size, value, **bits))
        cot_parts = []
        for clip, block in enumerate(part):
            at = clip * group
            cot_parts.append(block[rows:group])
            cot_parts += [array[at + rows : at + group] for array in near]
        swapped = exchange(size, jnp.concatenate(cot_parts), core=1)
        total = products(size, part, near, swapped, total)
    keep, send = total
    theirs = exchange(size, send, core=1)
    weight = (keep + theirs) / math.sqrt(size.total)
    weight = weight.transpose(0, 2, 1).reshape(TAPS, TAPS, TAPS, rows, size.narrow)
    return input_grad, weight


def solution(mesh):
    in_specs = (P("clip", "tm", "tile", None, None), P("clip", "tm", "tile", None, None), P())
    out_specs = (P("clip", "tm", "tile", None, None), P(None, None, None, "tile", ("clip", "tm")))

    def on_device(activation, cotangent, kernel_weight):
        size = Sizes(mesh.shape, activation.shape)
        if size.fits():
            return gather_plan(size, activation, cotangent, kernel_weight)
        return general_plan(activation, cotangent, kernel_weight)

    return jax.shard_map(
        on_device, mesh=mesh, in_specs=in_specs, out_specs=out_specs, check_vma=False
    )
```
